256 devices in a mesh: seq: 64 (over z, x, core), mp: 4 (over y).
Axes of the slice: x: 4, y: 4, z: 8, core: 2. Of those that a mesh axis runs over, the one named last changes fastest.
Arguments:
- span_pairs: bfloat16 [32768, 2, 896], P('seq', None, 'mp'), may hold values from -6 to 6
- dec_queries: bfloat16 [32768, 2048], P('seq', 'mp'), may hold values from -6 to 6
- database: float32 [128, 128, 896], P('seq'), may hold values from -6 to 6
- nbr_index: int32 [512, 2], P('seq'), may hold values from 0 to 1
- nbr_host: int32 [512, 2], P('seq'), may hold values from 0 to 63, as said below
- enc_gain: float32 [896], replicated, may hold values from 0.25 to 1.75
- enc_query: bfloat16 [896, 896], P(None, 'mp'), may hold values from -0.1875 to 0.1875
- enc_out: bfloat16 [896, 896], P('mp'), may hold values from -0.1875 to 0.1875
- ffn_gain: float32 [896], replicated, may hold values from 0.25 to 1.75
- ffn_up: bfloat16 [896, 1792], P(None, 'mp'), may hold values from -0.1875 to 0.1875
- ffn_down: bfloat16 [1792, 896], P('mp'), may hold values from -0.125 to 0.125
- dec_kv: bfloat16 [896, 2, 2048], P(None, None, 'mp'), may hold values from -0.1875 to 0.1875
Outputs:
- attended: float32 [32768, 2048], P('seq', 'mp')
The draws below stay inside these ranges and needn't reach their ends.
Inputs may be any that keep to these rules, and one draw needn't show every extreme that they name: `nbr_host`: the 16 neighbours of the spans of one seq index name each host at most 1 times, and some host exactly 1 times. Over all spans every host is named exactly 16 times.
All inputs are finite; a program needn't handle non-finite values.
Results may differ from the reference program's by a relative error of at most 0.019.
Values may be sent and summed in bfloat16 or wider, within the bound.
A program may use at most 128 MiB of HBM per device.

```python
import jax
import jax.numpy as jnp
from jax import lax

D = 2048
HEADS = 16
HEAD_DIM = 128
E = 896
EHEADS = 8
EHEAD_DIM = 112
FFE = 1792
SPAN = 64
NBL = 128
NEIGH = 2
DB_DEV = 2
CH_DEV = 8
SPANS = 512
TOKENS = 32768
DB_ROWS = 128
N_SEQ = 64
N_MP = 4


def host_table(key):
    inner_key = jax.random.fold_in(key, 17)
    relabel = jax.random.permutation(inner_key, N_SEQ)
    sources = jnp.arange(N_SEQ)[:, None]
    offsets = jnp.arange(NEIGH * CH_DEV)[None, :]
    nominal = (sources + offsets) % N_SEQ
    return relabel[nominal].astype(jnp.int32)


def draw_nbr_host(key, part):
    return host_table(key).reshape(N_SEQ * CH_DEV, NEIGH)


def place_ends(values, key, smallest, high):
    longest = values.shape.index(max(values.shape))
    spots = []
    for shift in (0, 1):
        where = [jax.random.randint(jax.random.fold_in(key, axis), (), 0, length) for axis, length in enumerate(values.shape)]
        where[longest] = (where[longest] + shift) % values.shape[longest]
        spots.append(tuple(where))
    return values.at[spots[0]].set(smallest).at[spots[1]].set(high)


def block_scale(stream_key, shape, pieces, smallest, top_value):
    def one(position, shards_of):
        heights = jax.random.uniform(jax.random.fold_in(jax.random.fold_in(stream_key, 6), position), (shards_of,), jnp.float32, smallest / len(pieces), top_value / len(pieces))
        return jnp.repeat(jnp.exp(heights), shape[position] // shards_of).reshape((-1,) + (1,) * (len(shape) - position - 1))

    level = one(*pieces[0])
    for cut in pieces[1:]:
        level = level * one(*cut)
    return level


def normal_values(key, extent, deviation, limit, shards=(), held_as=jnp.bfloat16):
    array = deviation * jax.random.normal(key, extent, jnp.float32)
    if shards:
        array = array * block_scale(key, extent, shards, -0.22, 0.18)
    return jnp.clip(array, -limit, limit).astype(held_as)


def setup_inputs(seed: int = 0) -> dict:
    arg_keys = jax.random.split(jax.random.key(seed), 13)
    return {
        "span_pairs": normal_values(arg_keys[0], (TOKENS, 2, E), 1.0, 6.0, ((0, 64), (2, 4))),
        "dec_queries": normal_values(arg_keys[1], (TOKENS, D), 1.0, 6.0, ((0, 64), (1, 4))),
        "database": normal_values(arg_keys[2], (DB_ROWS, NBL, E), 1.0, 6.0, ((0, 64),), jnp.float32),
        "nbr_index": place_ends(jax.random.randint(arg_keys[3], (SPANS, NEIGH), 0, DB_DEV), jax.random.fold_in(arg_keys[3], 1), 0, DB_DEV - 1).astype(jnp.int32),
        "nbr_host": draw_nbr_host(jax.random.fold_in(arg_keys[12], 71), 0),
        "enc_gain": jnp.clip(1.0 + 0.15 * jax.random.normal(arg_keys[5], (E,), jnp.float32), 0.25, 1.75),
        "enc_query": normal_values(arg_keys[6], (E, E), E ** -0.5, 0.1875, ((1, 4),)),
        "enc_out": normal_values(arg_keys[7], (E, E), E ** -0.5, 0.1875, ((0, 4),)),
        "ffn_gain": jnp.clip(1.0 + 0.15 * jax.random.normal(arg_keys[8], (E,), jnp.float32), 0.25, 1.75),
        "ffn_up": normal_values(arg_keys[9], (E, FFE), E ** -0.5, 0.1875, ((1, 4),)),
        "ffn_down": normal_values(arg_keys[10], (FFE, E), FFE ** -0.5, 0.125, ((0, 4),)),
        "dec_kv": normal_values(arg_keys[11], (E, 2, D), E ** -0.5, 0.1875, ((2, 4),)),
    }


def rms_scale(values, gain):
    return values * lax.rsqrt(lax.optimization_barrier(jnp.mean(values * values, axis=-1, keepdims=True)) + 1e-06) * gain

def reference(span_pairs, dec_queries, database, nbr_index, nbr_host, enc_gain, enc_query, enc_out, ffn_gain, ffn_up, ffn_down, dec_kv):
    enc_pairs = span_pairs.reshape(SPANS, SPAN, 2, E)
    entries = (nbr_host * DB_DEV + nbr_index).astype(jnp.int32)
    query_blocks = dec_queries.reshape(SPANS, SPAN, D)
    lane_width = E // N_MP
    unit_width = FFE // N_MP
    enc_scale = float(EHEAD_DIM) ** (-0.5)
    dec_scale = float(HEAD_DIM) ** (-0.5)
    out_groups = enc_out.reshape(N_MP, lane_width, E).astype(jnp.float32)
    down_groups = ffn_down.reshape(N_MP, unit_width, E).astype(jnp.float32)
    kv_flat = dec_kv.reshape(E, 2 * D)

    def one_span(inputs):
        rows, pairs, queries_in = inputs
        neighbours = jnp.take(database, rows, axis=0).reshape(NEIGH * NBL, E)
        normed = rms_scale(neighbours, enc_gain).astype(jnp.bfloat16)
        query = (jnp.dot(normed, enc_query, preferred_element_type=jnp.float32) * enc_scale).astype(jnp.bfloat16)
        query = query.reshape(NEIGH * NBL, EHEADS, EHEAD_DIM).astype(jnp.float32)
        keys = pairs[:, 0].reshape(SPAN, EHEADS, EHEAD_DIM).astype(jnp.float32)
        values = pairs[:, 1].reshape(SPAN, EHEADS, EHEAD_DIM).astype(jnp.float32)
        scores = jnp.einsum('rhd,khd->hrk', query, keys)
        weights = jax.nn.softmax(scores, axis=-1).astype(jnp.bfloat16)
        enc_attended = jnp.einsum('hrk,khd->rhd', weights.astype(jnp.float32), values).astype(jnp.bfloat16)
        enc_attended = enc_attended.reshape(NEIGH * NBL, N_MP, lane_width).astype(jnp.float32)
        partial_value = jnp.einsum('rgf,gfe->rge', enc_attended, out_groups).astype(jnp.bfloat16)
        resid = neighbours + lax.optimization_barrier(jnp.sum(partial_value.astype(jnp.float32), axis=1))
        inner = rms_scale(resid, ffn_gain).astype(jnp.bfloat16)
        units = jax.nn.gelu(jnp.dot(inner, ffn_up, preferred_element_type=jnp.float32)).astype(jnp.bfloat16)
        units = units.reshape(NEIGH * NBL, N_MP, unit_width).astype(jnp.float32)
        down_terms = jnp.einsum('rgf,gfe->rge', units, down_groups).astype(jnp.bfloat16)
        encoded = (resid + lax.optimization_barrier(jnp.sum(down_terms.astype(jnp.float32), axis=1))).astype(jnp.bfloat16)
        dec_pairs = jnp.dot(encoded, kv_flat, preferred_element_type=jnp.float32).astype(jnp.bfloat16)
        dec_pairs = dec_pairs.reshape(NEIGH * NBL, 2, HEADS, HEAD_DIM).astype(jnp.float32)
        dec_q = (queries_in.astype(jnp.float32) * dec_scale).astype(jnp.bfloat16)
        dec_q = dec_q.reshape(SPAN, HEADS, HEAD_DIM).astype(jnp.float32)
        dec_scores = jnp.einsum('qhd,khd->hqk', dec_q, dec_pairs[:, 0])
        dec_weights = jax.nn.softmax(dec_scores, axis=-1).astype(jnp.bfloat16)
        result = jnp.einsum('hqk,khd->qhd', dec_weights.astype(jnp.float32), dec_pairs[:, 1])
        return result.reshape(SPAN, D)
    outputs = lax.map(one_span, (entries[:-1], enc_pairs[:-1], query_blocks[1:]))
    first = jnp.zeros((1, SPAN, D), jnp.float32)
    return jnp.concatenate([first, outputs], axis=0).reshape(TOKENS, D)
```

```python
import jax
import jax.numpy as jnp
from jax import lax
from jax.experimental import pallas as pl
from jax.experimental.pallas import tpu as pltpu
from jax.sharding import PartitionSpec as P

HEAD_DIM = 128
EHEAD_DIM = 112
SPAN = 64
NBL = 128
NEIGH = 2
CH_DEV = 8
NZ, NX, NC, NY = 8, 4, 2, 4
E = 896
LANE = 224
UNIT = 448
DLANE = 512
QROWS = NBL // NY
ROWS = 2 * NEIGH * NBL
F32 = jnp.float32
BF16 = jnp.bfloat16
MESH_ID = pl.DeviceIdType.MESH
SEMS = 160


def rms_scale(values, gain):
    return values * lax.rsqrt(jnp.mean(values * values, axis=-1, keepdims=True) + 1e-06) * gain


class Net:
    def __init__(self, send_sem, recv_sem, copy_sem, any_dev):
        self.send_sem, self.recv_sem, self.copy_sem = send_sem, recv_sem, copy_sem
        self.any_dev = any_dev
        self.count = 0
        self.local_count = 0
        self.sent = []

    def number(self, many=1):
        first = self.count
        self.count += many
        return first

    def describe(self, src, dst, i, dev, j=None):
        return pltpu.make_async_remote_copy(
            src_ref=src,
            dst_ref=dst,
            send_sem=self.send_sem.at[i],
            recv_sem=self.recv_sem.at[i if j is None else j],
            device_id=dev,
            device_id_type=MESH_ID,
        )

    def send(self, src, dst, dev):
        i = self.number()
        copy = self.describe(src, dst, i, dev)
        copy.start()
        self.sent.append(copy)
        return i

    def recv(self, i, view):
        self.describe(view, view, i, self.any_dev).wait_recv()

    def local(self, src, dst):
        copy = pltpu.make_async_copy(src, dst, self.copy_sem.at[self.local_count])
        self.local_count += 1
        copy.start()
        return copy


class Ring:
    def __init__(self, net, n, p, right, left, views, halves):
        self.net, self.n, self.p = net, n, p
        self.right, self.left = right, left
        self.views, self.halves = views, halves
        self.numbers = None

    def first(self, sources=None):
        self.numbers = []
        for a, view in enumerate(self.views):
            own = view(self.p, slice(None))
            src = own if sources is None else sources[a]
            self.numbers.append((self.net.send(src, own, self.right), self.net.send(src, own, self.left)))

    def arrive(self, k):
        n, p = self.n, self.p
        before, after = lax.rem(p + n - k, n), lax.rem(p + k, n)
        last = k == n // 2
        numbers = []
        for a, view in enumerate(self.views):
            from_left, from_right = self.numbers[a]
            lo, hi = self.halves[a]
            self.net.recv(from_left, view(before, lo if last else slice(None)))
            self.net.recv(from_right, view(after, hi if last else slice(None)))
            if last:
                continue
            half = k + 1 == n // 2
            left_block = view(before, lo if half else slice(None))
            right_block = view(after, hi if half else slice(None))
            numbers.append(
                (
                    self.net.send(left_block, left_block, self.right),
                    self.net.send(right_block, right_block, self.left),
                )
            )
        self.numbers = numbers
        return before, after


def cut(rows, at):
    return pl.ds(0, at), pl.ds(at, rows - at)


def kernel(
    host_ref,
    index_ref,
    db_hbm,
    kv_hbm,
    q_hbm,
    wq_hbm,
    wo_hbm,
    up_hbm,
    dn_hbm,
    wb_hbm,
    gain_a,
    gain_b,
    out_ref,
    DB,
    WQ,
    WO,
    UP,
    DN,
    WB,
    KV,
    Q,
    SEL,
    EN,
    OUTB,
    NORM,
    ACC,
    ORECV,
    send_sem,
    recv_sem,
    copy_sem,
):
    seq = lax.axis_index("seq")
    y = lax.axis_index("mp")
    z, x, c = seq // (NX * NC), lax.rem(seq // NC, NX), lax.rem(seq, NC)

    def at(zz, xx, cc, yy):
        return ((zz * NX + xx) * NC + cc, yy)

    def lane(d):
        return lax.rem(y + d, NY)

    x_right, x_left = at(z, lax.rem(x + 1, NX), c, y), at(z, lax.rem(x + NX - 1, NX), c, y)
    z_right, z_left = at(lax.rem(z + 1, NZ), x, c, y), at(lax.rem(z + NZ - 1, NZ), x, c, y)
    y_right, y_left, y_far = (seq, lane(1)), (seq, lane(3)), (seq, lane(2))
    partner = at(z, x, 1 - c, y)
    seq_next, seq_prev = lax.rem(seq + 1, NZ * NX * NC), lax.rem(seq + NZ * NX * NC - 1, NZ * NX * NC)
    follow = (seq_next, 0)

    barrier = pltpu.get_barrier_semaphore()

    def greet(dev):
        pl.semaphore_signal(barrier, inc=1, device_id=dev, device_id_type=MESH_ID)

    for dev in (x_right, x_left, z_right, z_left, y_right, y_left, y_far, partner, follow):
        greet(dev)

    @pl.when(y == 0)
    def _():
        for g in range(NY):
            greet((seq_prev, g))
        pl.semaphore_wait(barrier, 8 + 1 + NY)

    @pl.when(y != 0)
    def _():
        pl.semaphore_wait(barrier, 8 + 1)

    net = Net(send_sem, recv_sem, copy_sem, partner)
    half16 = cut(32, 16)
    whole = slice(None)

    one_x = Ring(net, NX, x, x_right, x_left, [lambda p, r: DB.at[z, p, c, 0, r, :]], [half16])
    one_z = Ring(net, NZ, z, z_right, z_left, [lambda p, r: DB.at[p, :, c, 0, r, :]], [half16])
    two_z = Ring(net, NZ, z, z_right, z_left, [lambda p, r: DB.at[p, x, c, 1, r, :]], [half16])
    two_x = Ring(net, NX, x, x_right, x_left, [lambda p, r: DB.at[:, p, c, 1, r, :]], [half16])
    one_x.first([db_hbm.at[0]])
    two_z.first([db_hbm.at[1]])
    db_own = net.local(db_hbm, DB.at[z, x, c])

    early = []

    def to_lanes(src_two, src_one, dst_two, dst_one):
        first = net.number(3)
        for d in range(1, NY):
            dest, slot, i = lane(d), NY - d, first + d - 1

            @pl.when(dest != 0)
            def _():
                net.describe(src_two(2 * dest - 1), dst_two(slot), i, (seq, dest)).start()

            @pl.when(dest == 0)
            def _():
                net.describe(src_one(0), dst_one(slot, 1), i, (seq, dest)).start()

        tail = net.number(NY)
        net.describe(src_one(CH_DEV - 1), dst_one(y, 0), tail, follow, tail + y).start()
        return first, tail

    def lanes_arrived(first, tail, dst_two, dst_one):
        for d in range(1, NY):
            slot, i = NY - d, first + d - 1

            @pl.when(y != 0)
            def _():
                net.recv(i, dst_two(slot))

            @pl.when(y == 0)
            def _():
                net.recv(i, dst_one(slot, 1))

        @pl.when(y == 0)
        def _():
            for g in range(NY):
                net.recv(tail + g, dst_one(g, 0))

    def lanes_sent(first, tail, src_two, src_one):
        for d in range(1, NY):
            dest, i = lane(d), first + d - 1

            @pl.when(dest != 0)
            def _():
                net.describe(src_two(0), src_two(0), i, partner).wait_send()

            @pl.when(dest == 0)
            def _():
                net.describe(src_one(0), src_one(0), i, partner).wait_send()

        net.describe(src_one(0), src_one(0), tail, partner).wait_send()

    kv_src_two = lambda m: kv_hbm.at[:, pl.ds(m, 2)]
    kv_src_one = lambda m: kv_hbm.at[:, pl.ds(m, 1)]
    kv_dst_two = lambda slot: KV.at[slot]
    kv_dst_one = lambda slot, pos: KV.at[slot, :, pl.ds(pos, 1)]
    kv_numbers = to_lanes(kv_src_two, kv_src_one, kv_dst_two, kv_dst_one)
    kv_own = net.local(kv_hbm.at[:, pl.ds(2 * y, 1)], KV.at[0, :, pl.ds(1, 1)])

    @pl.when(y != 0)
    def _():
        pltpu.make_async_copy(
            kv_hbm.at[:, pl.ds(2 * y - 1, 1)], KV.at[0, :, pl.ds(0, 1)], copy_sem.at[40]
        ).start()

    piece = 2 * x + c
    low_piece = jnp.minimum(piece, 6)
    halves_a = [cut(112, 64), cut(32, 16), cut(112, 64), cut(64, 32)]
    bufs_a = [WQ, WO, UP, DN]
    srcs_a = [wq_hbm.at[x, c], wo_hbm.at[low_piece], up_hbm.at[x, c], dn_hbm.at[low_piece]]

    def y_first(buf, src, i, j):
        return net.send(src, buf.at[3, i, j], y_right), net.send(src, buf.at[1, i, j], y_left)

    def y_relay(buf, halves, numbers, i, j):
        lo, hi = halves
        net.recv(numbers[0], buf.at[3, i, j])
        a = net.send(buf.at[3, i, j, lo, :], buf.at[2, i, j, lo, :], y_right)
        net.recv(numbers[1], buf.at[1, i, j])
        b = net.send(buf.at[1, i, j, hi, :], buf.at[2, i, j, hi, :], y_left)
        return a, b

    def y_last(buf, halves, numbers, i, j):
        lo, hi = halves
        net.recv(numbers[0], buf.at[2, i, j, lo, :])
        net.recv(numbers[1], buf.at[2, i, j, hi, :])

    ya = [y_first(bufs_a[a], srcs_a[a], x, c) for a in range(4)]
    q_numbers = []
    for d in range(1, NY):
        q_numbers.append(
            net.send(q_hbm.at[pl.ds(lane(d) * 128, 128)], Q.at[NY - d], (seq, lane(d)))
        )
    yb = y_first(WB, wb_hbm.at[z, c], z, c)
    own = [
        net.local(wq_hbm, WQ.at[0]),
        net.local(up_hbm, UP.at[0]),
        net.local(wb_hbm, WB.at[0]),
        net.local(q_hbm.at[pl.ds(y * 128, 128)], Q.at[0]),
    ]
    for i in range(7):
        own.append(net.local(wo_hbm.at[i], WO.at[0, i // 2, i % 2]))
        own.append(net.local(dn_hbm.at[i], DN.at[0, i // 2, i % 2]))

    others = pl.ds(1, 3)

    def view_a(buf):
        return lambda p, r: buf.at[others, p, c, r, :]

    ring_qo = Ring(net, NX, x, x_right, x_left, [view_a(WQ), view_a(WO)], halves_a[:2])
    ring_ud = Ring(net, NX, x, x_right, x_left, [view_a(UP), view_a(DN)], halves_a[2:])
    ring_b = Ring(net, NZ, z, z_right, z_left, [view_a(WB)], [cut(112, 64)])

    across = []

    def share(view):
        across.append((net.send(view(c), view(c), partner), view))

    def shared_here(items):
        for i, view in items:
            net.recv(i, view(1 - c))

    one_x.arrive(1)
    two_z.arrive(1)
    db_own.wait()
    one_x.arrive(2)
    one_z.first()
    share(lambda s: DB.at[z, :, s, 0])
    two_z.arrive(2)
    two_z.arrive(3)
    ya[0] = y_relay(WQ, halves_a[0], ya[0], x, c)
    ya[1] = y_relay(WO, halves_a[1], ya[1], x, c)
    two_z.arrive(4)
    two_x.first()
    share(lambda s: DB.at[:, x, s, 1])

    def one_step(k):
        before, after = one_z.arrive(k)
        share(lambda s: DB.at[before, :, s, 0])
        if k < NZ // 2:
            share(lambda s: DB.at[after, :, s, 0])

    def two_step(k):
        before, after = two_x.arrive(k)
        share(lambda s: DB.at[:, before, s, 1])
        if k < NX // 2:
            share(lambda s: DB.at[:, after, s, 1])

    y_last(WQ, halves_a[0], ya[0], x, c)
    y_last(WO, halves_a[1], ya[1], x, c)
    ring_qo.first()
    one_step(1)
    ya[2] = y_relay(UP, halves_a[2], ya[2], x, c)
    ya[3] = y_relay(DN, halves_a[3], ya[3], x, c)
    one_step(2)
    two_step(1)
    yb = y_relay(WB, cut(112, 64), yb, z, c)
    y_last(UP, halves_a[2], ya[2], x, c)
    y_last(DN, halves_a[3], ya[3], x, c)
    ring_ud.first()
    one_step(3)
    y_last(WB, cut(112, 64), yb, z, c)
    ring_b.first()
    ring_qo.arrive(1)
    two_step(2)
    one_step(4)
    shared_here(across)
    db_across = len(across)

    for m in range(CH_DEV):
        for k in range(NEIGH):
            host = host_ref[m, k]
            SEL[m, k] = DB[host // (NX * NC), lax.rem(host // NC, NX), lax.rem(host, NC), index_ref[m, k]]
    e_src_two = lambda m: SEL.at[pl.ds(m, 2)]
    e_src_one = lambda m: SEL.at[pl.ds(m, 1)]
    e_dst_two = lambda slot: EN.at[:, slot]
    e_dst_one = lambda slot, pos: EN.at[pl.ds(pos, 1), slot]
    e_numbers = to_lanes(e_src_two, e_src_one, e_dst_two, e_dst_one)
    EN[1, 0] = SEL[2 * y]

    @pl.when(y != 0)
    def _():
        EN[0, 0] = SEL[2 * y - 1]

    ring_qo.arrive(2)
    share(lambda s: WQ.at[others, :, s])
    share(lambda s: WO.at[others, :, s])
    ring_ud.arrive(1)
    ring_b.arrive(1)
    lanes_arrived(*kv_numbers, kv_dst_two, kv_dst_one)
    kv_own.wait()

    @pl.when(y != 0)
    def _():
        pltpu.make_async_copy(
            kv_hbm.at[:, pl.ds(2 * y - 1, 1)], KV.at[0, :, pl.ds(0, 1)], copy_sem.at[40]
        ).wait()

    for copy in own:
        copy.wait()
    for d in range(1, NY):
        net.recv(q_numbers[d - 1], Q.at[NY - d])
    lanes_arrived(*e_numbers, e_dst_two, e_dst_one)

    neighbours = EN[...].reshape(ROWS, E).astype(F32)
    ACC[...] = neighbours
    NORM[...] = rms_scale(neighbours, gain_a[...]).astype(BF16)
    shared_here(across[db_across:])

    head_of_row = lax.broadcasted_iota(jnp.int32, (2 * SPAN, LANE), 0) >= SPAN
    head_of_lane = lax.broadcasted_iota(jnp.int32, (2 * SPAN, LANE), 1) >= EHEAD_DIM
    head_mask = jnp.where(head_of_row == head_of_lane, 1.0, 0.0).astype(BF16)
    last_last = (((1,), (1,)), ((), ()))
    first_first = (((0,), (0,)), ((), ()))

    def attend(k, carry):
        query = jnp.dot(NORM[...], WQ[k].reshape(E, LANE), preferred_element_type=F32)
        query = (query * float(EHEAD_DIM) ** -0.5).astype(BF16)
        w_out = WO[k].reshape(256, E)[:LANE]
        for pos in range(2):
            keys = KV[k, 0, pos]
            values = KV[k, 1, pos]
            keys = jnp.concatenate([keys, keys], axis=0) * head_mask
            values = jnp.concatenate([values, values], axis=0) * head_mask
            mine = query[pos * 256 : (pos + 1) * 256]
            scores = lax.dot_general(keys, mine, last_last, preferred_element_type=F32)
            scores = scores.reshape(2, SPAN, 256)
            top = jnp.max(scores, axis=1, keepdims=True)
            parts = jnp.exp(scores - top)
            parts = parts / jnp.sum(parts, axis=1, keepdims=True)
            weights = parts.reshape(2 * SPAN, 256).astype(BF16)
            got = lax.dot_general(weights, values, first_first, preferred_element_type=F32)
            ACC[pl.ds(pos * 256, 256), :] += jnp.dot(
                got.astype(BF16), w_out, preferred_element_type=F32
            )
        return carry

    lax.fori_loop(0, NY, attend, 0)
    ring_ud.arrive(2)
    ud = len(across)
    share(lambda s: UP.at[others, :, s])
    share(lambda s: DN.at[others, :, s])
    ring_b.arrive(2)
    NORM[...] = rms_scale(ACC[...], gain_b[...]).astype(BF16)
    shared_here(across[ud:])

    def feed(k, carry):
        units = jnp.dot(NORM[...], UP[k].reshape(E, UNIT), preferred_element_type=F32)
        units = jax.nn.gelu(units).astype(BF16)
        ACC[...] += jnp.dot(units, DN[k].reshape(512, E)[:UNIT], preferred_element_type=F32)
        return carry

    lax.fori_loop(0, 2, feed, 0)
    ring_b.arrive(3)
    lax.fori_loop(2, NY, feed, 0)
    NORM[...] = ACC[...].astype(BF16)
    ring_b.arrive(4)
    share(lambda s: WB.at[others, :, s])
    shared_here(across[-1:])

    o_first = net.number(NY)

    def decode(i, carry):
        k = lax.rem(i + 1, NY)
        keys = jnp.dot(NORM[...], WB[k, 0:4].reshape(E, DLANE), preferred_element_type=F32)
        keys = keys.astype(BF16)
        values = jnp.dot(NORM[...], WB[k, 4:8].reshape(E, DLANE), preferred_element_type=F32)
        values = values.astype(BF16)
        queries = (Q[k].astype(F32) * float(HEAD_DIM) ** -0.5).astype(BF16)
        for pos in range(2):
            for h in range(4):
                cols = slice(h * HEAD_DIM, (h + 1) * HEAD_DIM)
                rows = slice(pos * 256, (pos + 1) * 256)
                toks = slice(pos * SPAN, (pos + 1) * SPAN)
                scores = lax.dot_general(
                    queries[toks, cols], keys[rows, cols], last_last, preferred_element_type=F32
                )
                top = jnp.max(scores, axis=1, keepdims=True)
                parts = jnp.exp(scores - top)
                parts = parts / jnp.sum(parts, axis=1, keepdims=True)
                got = jnp.dot(parts.astype(BF16), values[rows, cols], preferred_element_type=F32)
                OUTB[k, toks, cols] = got.astype(BF16)

        @pl.when(k != 0)
        def _():
            net.describe(OUTB.at[k], ORECV.at[y], o_first + k, (seq, lane(k))).start()

        return carry

    lax.fori_loop(0, NY, decode, 0)
    out_ref[y] = OUTB[0]
    for k in range(1, NY):
        source = lane(NY - k)
        net.recv(o_first + k, ORECV.at[source])
        out_ref[source] = ORECV[source]
    for k in range(1, NY):
        net.describe(OUTB.at[k], OUTB.at[k], o_first + k, partner).wait_send()
    lanes_sent(*kv_numbers, kv_src_two, kv_src_one)
    lanes_sent(*e_numbers, e_src_two, e_src_one)
    for copy in net.sent:
        copy.wait_send()
    assert net.count <= SEMS and net.local_count <= 40


def on_device(
    span_pairs,
    dec_queries,
    database,
    nbr_index,
    nbr_host,
    enc_gain,
    enc_query,
    enc_out,
    ffn_gain,
    ffn_up,
    ffn_down,
    dec_kv,
):
    y = lax.axis_index("mp")
    seq = lax.axis_index("seq")
    db = lax.dynamic_slice_in_dim(database, y * QROWS, QROWS, 1).astype(BF16)
    kv = jnp.moveaxis(span_pairs, 1, 0).reshape(2, CH_DEV, SPAN, LANE)
    wb = jnp.moveaxis(dec_kv, 1, 0).reshape(NZ, NC, 112, DLANE)
    anywhere = pl.BlockSpec(memory_space=pl.ANY)
    in_smem = pl.BlockSpec(memory_space=pltpu.SMEM)
    in_vmem = pl.BlockSpec(memory_space=pltpu.VMEM)
    got = pl.pallas_call(
        kernel,
        out_shape=jax.ShapeDtypeStruct((NY, 128, DLANE), BF16),
        in_specs=[in_smem] * 2 + [anywhere] * 8 + [in_vmem] * 2,
        out_specs=in_vmem,
        scratch_shapes=[
            pltpu.VMEM((NZ, NX, NC, 2, QROWS, E), BF16),
            pltpu.VMEM((NY, NX, NC, 112, LANE), BF16),
            pltpu.VMEM((NY, NX, NC, 32, E), BF16),
            pltpu.VMEM((NY, NX, NC, 112, UNIT), BF16),
            pltpu.VMEM((NY, NX, NC, 64, E), BF16),
            pltpu.VMEM((NY, NZ, NC, 112, DLANE), BF16),
            pltpu.VMEM((NY, 2, 2, SPAN, LANE), BF16),
            pltpu.VMEM((NY, 128, DLANE), BF16),
            pltpu.VMEM((CH_DEV, NEIGH, QROWS, E), BF16),
            pltpu.VMEM((2, NY, NEIGH, QROWS, E), BF16),
            pltpu.VMEM((NY, 128, DLANE), BF16),
            pltpu.VMEM((ROWS, E), BF16),
            pltpu.VMEM((ROWS, E), F32),
            pltpu.VMEM((NY, 128, DLANE), BF16),
            pltpu.SemaphoreType.DMA((SEMS,)),
            pltpu.SemaphoreType.DMA((SEMS,)),
            pltpu.SemaphoreType.DMA((41,)),
        ],
        compiler_params=pltpu.CompilerParams(
            collective_id=0, has_side_effects=True, vmem_limit_bytes=63 * 1024 * 1024
        ),
    )(
        nbr_host,
        nbr_index,
        db,
        kv,
        dec_queries,
        enc_query.reshape(NX, NC, 112, LANE),
        enc_out.reshape(7, 32, E),
        ffn_up.reshape(NX, NC, 112, UNIT),
        ffn_down.reshape(7, 64, E),
        wb,
        enc_gain.reshape(1, E),
        ffn_gain.reshape(1, E),
    )
    got = got.reshape(CH_DEV * SPAN, DLANE).astype(F32)
    token = lax.broadcasted_iota(jnp.int32, got.shape, 0)
    return jnp.where((seq == 0) & (token < SPAN), 0.0, got)


def solution(mesh):
    placed = (
        P("seq", None, "mp"),
        P("seq", "mp"),
        P("seq", None, None),
        P("seq", None),
        P("seq", None),
        P(),
        P(None, "mp"),
        P("mp", None),
        P(),
        P(None, "mp"),
        P("mp", None),
        P(None, None, "mp"),
    )
    return jax.shard_map(
        on_device, mesh=mesh, in_specs=placed, out_specs=P("seq", "mp"), check_vma=False
    )
```
